32 devices in a mesh: groups: 2 (over y), row: 16 (over z, x, core).
Axes of the slice: x: 2, y: 2, z: 4, core: 2. Of those that a mesh axis runs over, the one named last changes fastest.
Arguments:
- strain_data: float32 [32, 32, 24576], P('row', None, 'groups'), parts along dimension 2, may hold values from -6 to 6
Outputs:
- coherence: float32 [2, 24576, 12288], P(None, ('groups', 'row')), parts along dimension 1
The draws below stay inside these ranges and needn't reach their ends.
There are 2 independent parts, one for each index of `groups`. The reference program is written for one: setup_inputs(seed, part) draws one part's arguments, and reference() takes and returns one part's arrays. A program takes and returns all parts, laid end to end along the dimension named above; each array names one. Nothing has to cross between parts.
All inputs are finite; a program needn't handle non-finite values.
Results may differ from the reference program's by a relative error of at most 0.00008.
Values sent between devices are 32-bit elements; how exact they have to be, the bound alone decides.
No kernel may reach another device: no remote copies, remote signals or barrier semaphores. Data moves between devices by JAX's collectives and lax.ppermute only.
A program may use at most 256 MiB of HBM per device.

```python
import jax
import jax.numpy as jnp
from jax import lax

CHANNELS = 12288
SAMPLES = 32
FBIN = 5
PANES = 32


def block_levels(stream_key, dims, pieces, smallest, largest):
    loudness = 1.0
    for axis_at, blocks in pieces:
        heights = jax.random.uniform(jax.random.fold_in(jax.random.fold_in(stream_key, 6), axis_at), (blocks,), jnp.float32, smallest / len(pieces), largest / len(pieces))
        loudness = loudness * jnp.repeat(jnp.exp(heights), dims[axis_at] // blocks).reshape((-1,) + (1,) * (len(dims) - 1 - axis_at))
    return loudness


def gaussian(rng, extent, width, reach, cuts=(), held_as=jnp.bfloat16):
    entries = jax.random.normal(rng, extent, jnp.float32) * width
    if len(cuts) > 0:
        entries = block_levels(rng, extent, cuts, -0.22, 0.18) * entries
    return jnp.clip(entries, min=-reach, max=reach).astype(held_as)


def setup_inputs(seed: int = 0, part: int = 0) -> dict:
    key_list = jax.random.split(jax.random.key(seed), 2)
    own_keys = jax.random.split(jax.random.fold_in(key_list[1], part), 2)
    strain_data = gaussian(own_keys[0], (PANES, SAMPLES, CHANNELS), 1.0, 6.0, ((0, 16),), jnp.float32)
    return {"strain_data": strain_data}


def project(strain_data):
    samples = strain_data.shape[1]
    position = jnp.arange(samples, dtype=jnp.float32)
    taper = 0.5 - 0.5 * jnp.cos(2.0 * jnp.pi * (position + 0.5) / samples)
    phase = 2.0 * jnp.pi * FBIN * position / samples
    weights = jnp.stack([taper * jnp.cos(phase), -taper * jnp.sin(phase)])
    rms = jnp.sqrt(lax.optimization_barrier(jnp.mean(strain_data * strain_data, axis=1, keepdims=True)))
    normed = strain_data / jnp.maximum(rms, 1.0)
    return jnp.einsum('ks,psc->kpc', weights, normed, precision=lax.Precision.HIGHEST)

def cross(left, right):
    real_part = jnp.einsum('pa,pb->ab', left[0], right[0], precision=lax.Precision.HIGHEST) + jnp.einsum('pa,pb->ab', left[1], right[1], precision=lax.Precision.HIGHEST)
    imag_part = jnp.einsum('pa,pb->ab', left[1], right[0], precision=lax.Precision.HIGHEST) - jnp.einsum('pa,pb->ab', left[0], right[1], precision=lax.Precision.HIGHEST)
    return jnp.stack([real_part, imag_part])

def reference(strain_data):
    spectrum = project(strain_data)
    power = lax.optimization_barrier(jnp.sum(spectrum * spectrum, axis=(0, 1)))
    scale = lax.rsqrt(power + 1e-06)
    return cross(spectrum, spectrum) * scale[None, :, None] * scale[None, None, :]
```

```python
import functools

import jax
import jax.numpy as jnp
import numpy as np
from jax import lax
from jax.experimental import pallas as pl
from jax.experimental.pallas import tpu as pltpu
from jax.sharding import PartitionSpec as P

FBIN = 5
LANES = 128
IN_VMEM = pl.BlockSpec(memory_space=pltpu.VMEM)


def project(strain_data):
    samples = strain_data.shape[1]
    position = jnp.arange(samples, dtype=jnp.float32)
    taper = 0.5 - 0.5 * jnp.cos(2.0 * jnp.pi * (position + 0.5) / samples)
    phase = 2.0 * jnp.pi * FBIN * position / samples
    weights = jnp.stack([taper * jnp.cos(phase), -taper * jnp.sin(phase)])
    rms = jnp.sqrt(jnp.mean(strain_data * strain_data, axis=1, keepdims=True))
    normed = strain_data / jnp.maximum(rms, 1.0)
    return jnp.einsum("ks,psc->kpc", weights, normed, precision=lax.Precision.HIGHEST)


def cross(left, right):
    real_part = jnp.einsum(
        "pa,pb->ab", left[0], right[0], precision=lax.Precision.HIGHEST
    ) + jnp.einsum("pa,pb->ab", left[1], right[1], precision=lax.Precision.HIGHEST)
    imag_part = jnp.einsum(
        "pa,pb->ab", left[1], right[0], precision=lax.Precision.HIGHEST
    ) - jnp.einsum("pa,pb->ab", left[0], right[1], precision=lax.Precision.HIGHEST)
    return jnp.stack([real_part, imag_part])


def gathered_form(strain_data):
    spectrum = project(strain_data)
    width = strain_data.shape[2] // lax.axis_size("row")
    offset = lax.axis_index("row") * width
    gathered = lax.all_gather(spectrum, "row", axis=1, tiled=True)
    own_rows = lax.dynamic_slice_in_dim(gathered, offset, width, 2)
    scale = lax.rsqrt(jnp.sum(gathered * gathered, axis=(0, 1)) + 1e-06)
    own_scale = lax.dynamic_slice_in_dim(scale, offset, width, 0)
    return (
        cross(own_rows, gathered) * own_scale[None, :, None] * scale[None, None, :]
    )


def tap_weights(samples):
    at = lax.broadcasted_iota(jnp.int32, (samples, LANES), 0)
    turn = 2.0 * np.pi / samples
    taper = 0.5 - 0.5 * jnp.cos((at.astype(jnp.float32) + 0.5) * turn)
    phase = ((at * FBIN) % samples).astype(jnp.float32) * turn
    return taper * jnp.cos(phase), -taper * jnp.sin(phase)


def project_kernel(other, row_ref, strain_ref, out_ref, held, arrived):
    blocks, panes, samples, width = held.shape
    parity = row_ref[0] & 1
    parity = 1 - parity if other else parity
    copies = []
    for i in range(blocks):
        start = pl.multiple_of((2 * i + parity) * width, width)
        copies.append(
            pltpu.make_async_copy(
                strain_ref.at[:, :, pl.ds(start, width)], held.at[i], arrived.at[i]
            )
        )
        copies[-1].start()
    weights = tap_weights(samples)
    for i in range(blocks):
        copies[i].wait()
        for lane in range(0, width, LANES):
            parts = [[], []]
            for p in range(panes):
                x = held[i, p, :, lane : lane + LANES]
                mean = jnp.sum(x * x, axis=0, keepdims=True) * (1.0 / samples)
                gain = 1.0 / jnp.maximum(jnp.sqrt(mean), 1.0)
                for k in range(2):
                    total = jnp.sum(x * weights[k], axis=0, keepdims=True)
                    parts[k].append(total * gain)
            at = i * width + lane
            out_ref[:, at : at + LANES] = jnp.concatenate(parts[0] + parts[1], axis=0)


def project_parity(row, strain_data, width, other):
    panes, samples, channels = strain_data.shape
    blocks = channels // (2 * width)
    return pl.pallas_call(
        functools.partial(project_kernel, other),
        grid_spec=pltpu.PrefetchScalarGridSpec(
            num_scalar_prefetch=1,
            grid=(1,),
            in_specs=[pl.BlockSpec(memory_space=pltpu.HBM)],
            out_specs=IN_VMEM,
            scratch_shapes=[
                pltpu.VMEM((blocks, panes, samples, width), jnp.float32),
                pltpu.SemaphoreType.DMA((blocks,)),
            ],
        ),
        out_shape=jax.ShapeDtypeStruct((2 * panes, blocks * width), jnp.float32),
        cost_estimate=pl.CostEstimate(
            flops=3 * strain_data.size,
            bytes_accessed=2 * strain_data.size,
            transcendentals=0,
        ),
        compiler_params=pltpu.CompilerParams(vmem_limit_bytes=62 << 20),
        name="project_other" if other else "project_own",
    )(row, strain_data)


def core_order(a, b, flip):
    return jnp.where(
        flip == 0,
        jnp.concatenate([a, b], axis=0),
        jnp.concatenate([b, a], axis=0),
    )


def pack_kernel(row_ref, *refs):
    flip = row_ref[0] & 1
    out_ref = refs[-1]
    rows = refs[0].shape[0]
    for i in range(0, len(refs) - 1, 2):
        out_ref[i * rows : (i + 2) * rows, :] = core_order(
            refs[i][...], refs[i + 1][...], flip
        )


def pack(row, pairs):
    arrays = [x for pair in pairs for x in pair]
    rows, columns = arrays[0].shape
    total = rows * len(arrays)
    return pl.pallas_call(
        pack_kernel,
        grid_spec=pltpu.PrefetchScalarGridSpec(
            num_scalar_prefetch=1,
            grid=(1,),
            in_specs=[IN_VMEM] * len(arrays),
            out_specs=IN_VMEM,
        ),
        out_shape=jax.ShapeDtypeStruct((total, columns), jnp.float32),
        cost_estimate=pl.CostEstimate(
            flops=total * columns, bytes_accessed=8 * total * columns, transcendentals=0
        ),
        compiler_params=pltpu.CompilerParams(vmem_limit_bytes=8 << 20),
    )(row, *arrays)


def scaled_rows(refs, block, width, flip):
    columns = pl.ds(pl.multiple_of(block * width, width), width)
    *packed, tail_a, tail_b = refs
    rows = jnp.concatenate(
        [x[:, columns] for x in packed]
        + [core_order(tail_a[:, columns], tail_b[:, columns], flip)],
        axis=0,
    )
    return rows * lax.rsqrt(jnp.sum(rows * rows, axis=0, keepdims=True) + 1e-06)


def halves(x):
    high = x.astype(jnp.bfloat16)
    low = (x - high.astype(jnp.float32)).astype(jnp.bfloat16)
    return high, low


def left_operand(x, panes):
    count = x.shape[0]
    row = lax.broadcasted_iota(jnp.int32, x.shape, 0) % (2 * panes)
    turned = jnp.where(
        row < panes, pltpu.roll(x, count - panes, 0), -pltpu.roll(x, panes, 0)
    )
    sides = []
    for rows in (x, turned):
        twice = jnp.concatenate([rows, rows], axis=0).T
        high, low = halves(twice)
        sides.append(jnp.concatenate([high, low], axis=1))
    return sides


def cross_kernel(first, panes, count, row_ref, *refs):
    parity = row_ref[0] & 1
    flip = parity if first else 1 - parity
    if first:
        right = refs[:count]
        out_ref, left_ref, right_ref = refs[count:]

        @pl.when(pl.program_id(0) == 0)
        def _():
            own = scaled_rows(right, row_ref[0] >> 1, left_ref.shape[1], flip)
            real, imag = left_operand(own, panes)
            left_ref[0] = real
            left_ref[1] = imag

    else:
        left_ref, right = refs[0], refs[1 : count + 1]
        out_ref, right_ref = refs[count + 2 :]

    width = out_ref.shape[2]
    high, low = halves(scaled_rows(right, pl.program_id(0), width, flip))
    rows = high.shape[0]
    for i, part in enumerate((high, low, high, low)):
        right_ref[i * rows : (i + 1) * rows, :] = part
    for part in range(2):
        out_ref[part] = jnp.dot(
            left_ref[part], right_ref[...], preferred_element_type=jnp.float32
        )


def cross_half(row, panes, width, columns, right, left=None, out=None):
    first = out is None
    rows = sum(x.shape[0] for x in right)
    blocks = right[0].shape[1] // width

    def out_block(i, row_ref):
        parity = row_ref[0] & 1
        return 0, 0, 2 * i + (parity if first else 1 - parity)

    in_specs = [IN_VMEM] * len(right)
    out_specs = pl.BlockSpec((2, width, width), out_block)
    out_shape = jax.ShapeDtypeStruct((2, width, columns), jnp.float32)
    operands, aliases = right, {}
    if first:
        out_specs = (out_specs, IN_VMEM)
        out_shape = (
            out_shape,
            jax.ShapeDtypeStruct((2, width, 4 * rows), jnp.bfloat16),
        )
    else:
        in_specs = [IN_VMEM, *in_specs, pl.BlockSpec(memory_space=pl.ANY)]
        operands = (left, *right, out)
        aliases = {len(operands): 0}
    return pl.pallas_call(
        functools.partial(cross_kernel, first, panes, len(right)),
        grid_spec=pltpu.PrefetchScalarGridSpec(
            num_scalar_prefetch=1,
            grid=(blocks,),
            in_specs=in_specs,
            out_specs=out_specs,
            scratch_shapes=[pltpu.VMEM((4 * rows, width), jnp.bfloat16)],
        ),
        out_shape=out_shape,
        input_output_aliases=aliases,
        cost_estimate=pl.CostEstimate(
            flops=8 * rows * width * columns,
            bytes_accessed=4 * width * columns,
            transcendentals=0,
        ),
        compiler_params=pltpu.CompilerParams(vmem_limit_bytes=32 << 20),
        name="cross_own" if first else "cross_other",
    )(row, *operands)


def ring_form(strain_data, ring):
    panes, _, channels = strain_data.shape
    chips = len(ring)
    width = channels // (2 * chips)
    up = [
        (2 * ring[i] + core, 2 * ring[(i + 1) % chips] + core)
        for core in range(2)
        for i in range(chips)
    ]
    down = [(b, a) for a, b in up]
    swap = [(i, i ^ 1) for i in range(2 * chips)]
    row = lax.axis_index("row").astype(jnp.int32).reshape(1)

    own = project_parity(row, strain_data, width, False)
    other = project_parity(row, strain_data, width, True)
    sibling = lax.ppermute(other, "row", swap)

    full = (chips - 1) // 2
    ups, downs = [(own, sibling)], [(own, sibling)]
    for _ in range(full):
        ups.append(tuple(lax.ppermute(x, "row", up) for x in ups[-1]))
        downs.append(tuple(lax.ppermute(x, "row", down) for x in downs[-1]))
    tail_a = lax.ppermute(ups[-1][0], "row", up)
    tail_b = lax.ppermute(downs[-1][1], "row", down)

    packed = pack(row, ups + downs[1:])
    mine = (packed, tail_a, tail_b)
    theirs = tuple(lax.ppermute(x, "row", swap) for x in mine)
    out, left = cross_half(row, panes, width, channels, mine)
    return cross_half(row, panes, width, channels, theirs, left, out)


def chip_ring(mesh):
    axes = list(mesh.axis_names)
    devices = np.moveaxis(mesh.devices, axes.index("row"), 0).reshape(
        mesh.shape["row"], -1
    )[::2, 0]
    order = list(range(len(devices)))
    if not all(hasattr(d, "coords") for d in devices):
        return order
    spots = [tuple(d.coords) for d in devices]
    varying = [a for a in range(len(spots[0])) if len({s[a] for s in spots}) > 1]
    if len(varying) != 2:
        return order
    short, long = sorted(varying, key=lambda a: len({s[a] for s in spots}))

    def key(i):
        at, along = spots[i][short], spots[i][long]
        return at, along if at % 2 == 0 else -along

    return sorted(order, key=key)


def solution(mesh):
    devices = mesh.shape["row"]
    ring = chip_ring(mesh)

    def on_device(strain_data):
        panes, _, channels = strain_data.shape
        width = channels // devices
        fits = (
            devices % 4 == 0
            and devices >= 8
            and width % LANES == 0
            and (4 * panes) % 8 == 0
        )
        if not fits:
            return gathered_form(strain_data)
        return ring_form(strain_data, ring)

    return jax.shard_map(
        on_device,
        mesh=mesh,
        in_specs=(P("row", None, "groups"),),
        out_specs=P(None, ("groups", "row"), None),
        check_vma=False,
    )
```

```python
import functools

import jax
import jax.numpy as jnp
import numpy as np
from jax import lax
from jax.experimental import pallas as pl
from jax.experimental.pallas import tpu as pltpu
from jax.sharding import PartitionSpec as P

FBIN = 5
LANES = 128
IN_VMEM = pl.BlockSpec(memory_space=pltpu.VMEM)


def project(strain_data):
    samples = strain_data.shape[1]
    position = jnp.arange(samples, dtype=jnp.float32)
    taper = 0.5 - 0.5 * jnp.cos(2.0 * jnp.pi * (position + 0.5) / samples)
    phase = 2.0 * jnp.pi * FBIN * position / samples
    weights = jnp.stack([taper * jnp.cos(phase), -taper * jnp.sin(phase)])
    rms = jnp.sqrt(jnp.mean(strain_data * strain_data, axis=1, keepdims=True))
    normed = strain_data / jnp.maximum(rms, 1.0)
    return jnp.einsum("ks,psc->kpc", weights, normed, precision=lax.Precision.HIGHEST)


def cross(left, right):
    real_part = jnp.einsum(
        "pa,pb->ab", left[0], right[0], precision=lax.Precision.HIGHEST
    ) + jnp.einsum("pa,pb->ab", left[1], right[1], precision=lax.Precision.HIGHEST)
    imag_part = jnp.einsum(
        "pa,pb->ab", left[1], right[0], precision=lax.Precision.HIGHEST
    ) - jnp.einsum("pa,pb->ab", left[0], right[1], precision=lax.Precision.HIGHEST)
    return jnp.stack([real_part, imag_part])


def gathered_form(strain_data):
    spectrum = project(strain_data)
    width = strain_data.shape[2] // lax.axis_size("row")
    offset = lax.axis_index("row") * width
    gathered = lax.all_gather(spectrum, "row", axis=1, tiled=True)
    own_rows = lax.dynamic_slice_in_dim(gathered, offset, width, 2)
    scale = lax.rsqrt(jnp.sum(gathered * gathered, axis=(0, 1)) + 1e-06)
    own_scale = lax.dynamic_slice_in_dim(scale, offset, width, 0)
    return (
        cross(own_rows, gathered) * own_scale[None, :, None] * scale[None, None, :]
    )


def tap_weights(samples):
    at = lax.broadcasted_iota(jnp.int32, (samples, LANES), 0)
    turn = 2.0 * np.pi / samples
    taper = 0.5 - 0.5 * jnp.cos((at.astype(jnp.float32) + 0.5) * turn)
    phase = ((at * FBIN) % samples).astype(jnp.float32) * turn
    return taper * jnp.cos(phase), -taper * jnp.sin(phase)


def project_kernel(strain_ref, out_ref, held, arrived):
    pieces, panes, samples, width = held.shape
    copies = [
        pltpu.make_async_copy(
            strain_ref.at[:, :, pl.ds(i * width, width)], held.at[i], arrived.at[i]
        )
        for i in range(pieces)
    ]
    for copy in copies:
        copy.start()
    weights = tap_weights(samples)
    for i in range(pieces):
        copies[i].wait()
        for lane in range(0, width, LANES):
            parts = [[], []]
            for p in range(panes):
                x = held[i, p, :, lane : lane + LANES]
                mean = jnp.sum(x * x, axis=0, keepdims=True) * (1.0 / samples)
                gain = jnp.minimum(lax.rsqrt(mean), 1.0)
                for k in range(2):
                    total = jnp.sum(x * weights[k], axis=0, keepdims=True)
                    parts[k].append(total * gain)
            at = i * width + lane
            out_ref[:, at : at + LANES] = jnp.concatenate(parts[0] + parts[1], axis=0)


def project_rows(strain_data, pieces):
    panes, samples, channels = strain_data.shape
    strain_data = pltpu.with_memory_space_constraint(strain_data, pltpu.HBM)
    return pl.pallas_call(
        project_kernel,
        in_specs=[pl.BlockSpec(memory_space=pltpu.HBM)],
        out_specs=IN_VMEM,
        scratch_shapes=[
            pltpu.VMEM((pieces, panes, samples, channels // pieces), jnp.float32),
            pltpu.SemaphoreType.DMA((pieces,)),
        ],
        out_shape=jax.ShapeDtypeStruct((2 * panes, channels), jnp.float32),
        cost_estimate=pl.CostEstimate(
            flops=6 * strain_data.size,
            bytes_accessed=4 * strain_data.size,
            transcendentals=0,
        ),
        compiler_params=pltpu.CompilerParams(vmem_limit_bytes=8 << 20),
        name="project",
    )(strain_data)


def scaled_rows(refs, block, width):
    columns = pl.ds(pl.multiple_of(block * width, width), width)
    rows = jnp.concatenate([x[:, columns] for x in refs], axis=0)
    return rows * lax.rsqrt(jnp.sum(rows * rows, axis=0, keepdims=True) + 1e-06)


def halves(x):
    high = x.astype(jnp.bfloat16)
    low = (x - high.astype(jnp.float32)).astype(jnp.bfloat16)
    return high, low


def left_operand(x, panes):
    count = x.shape[0]
    row = lax.broadcasted_iota(jnp.int32, x.shape, 0) % (2 * panes)
    turned = jnp.where(
        row < panes, pltpu.roll(x, count - panes, 0), -pltpu.roll(x, panes, 0)
    )
    sides = []
    for rows in (x, turned):
        twice = jnp.concatenate([rows, rows], axis=0).T
        high, low = halves(twice)
        sides.append(jnp.concatenate([high, low], axis=1))
    return sides


def cross_kernel(panes, row_ref, *refs):
    *spectra, out_ref, left_ref, right_ref = refs
    width = out_ref.shape[2]

    @pl.when(pl.program_id(0) == 0)
    def _():
        own = scaled_rows(spectra, row_ref[0], width)
        for part, rows in enumerate(left_operand(own, panes)):
            left_ref[part] = rows

    high, low = halves(scaled_rows(spectra, pl.program_id(0), width))
    count = high.shape[0]
    for i, part in enumerate((high, low, high, low)):
        right_ref[i * count : (i + 1) * count, :] = part
    for part in range(2):
        out_ref[part] = jnp.dot(
            left_ref[part], right_ref[...], preferred_element_type=jnp.float32
        )


def cross_rows(row, panes, width, spectra):
    columns = spectra[0].shape[1]
    count = sum(x.shape[0] for x in spectra)
    return pl.pallas_call(
        functools.partial(cross_kernel, panes),
        grid_spec=pltpu.PrefetchScalarGridSpec(
            num_scalar_prefetch=1,
            grid=(columns // width,),
            in_specs=[IN_VMEM] * len(spectra),
            out_specs=pl.BlockSpec((2, width, width), lambda i, row_ref: (0, 0, i)),
            scratch_shapes=[
                pltpu.VMEM((2, width, 4 * count), jnp.bfloat16),
                pltpu.VMEM((4 * count, width), jnp.bfloat16),
            ],
        ),
        out_shape=jax.ShapeDtypeStruct((2, width, columns), jnp.float32),
        cost_estimate=pl.CostEstimate(
            flops=16 * count * width * columns,
            bytes_accessed=8 * width * columns,
            transcendentals=0,
        ),
        compiler_params=pltpu.CompilerParams(vmem_limit_bytes=36 << 20),
        name="cross",
    )(row, *spectra)


def move(x, pairs):
    return lax.ppermute(x, "row", pairs)


def ring_form(strain_data, ring):
    panes, _, channels = strain_data.shape
    chips = len(ring)
    width = channels // (2 * chips)
    hop = []
    for i in range(chips):
        here, there = ring[i], ring[(i + 1) % chips]
        hop += [(2 * here, 2 * there), (2 * there + 1, 2 * here + 1)]
    swap = [(i, i ^ 1) for i in range(2 * chips)]
    row = lax.axis_index("row").astype(jnp.int32).reshape(1)

    own = project_rows(strain_data, chips)
    sibling = move(own, swap)
    spectra = [own, sibling]
    a, b = own, sibling
    for _ in range(1, (chips - 1) // 2 + 1):
        a = move(a, hop)
        b = move(b, hop)
        spectra += [a, b]
        spectra += [move(a, swap), move(b, swap)]
    tail = move(a, hop)
    spectra += [tail, move(tail, swap)]
    return cross_rows(row, panes, width, spectra)


def chip_ring(mesh):
    axes = list(mesh.axis_names)
    devices = np.moveaxis(mesh.devices, axes.index("row"), 0).reshape(
        mesh.shape["row"], -1
    )[::2, 0]
    order = list(range(len(devices)))
    if not all(hasattr(d, "coords") for d in devices):
        return order
    spots = [tuple(d.coords) for d in devices]
    varying = [a for a in range(len(spots[0])) if len({s[a] for s in spots}) > 1]
    if len(varying) != 2:
        return order
    short, long = sorted(varying, key=lambda a: len({s[a] for s in spots}))

    def key(i):
        at, along = spots[i][short], spots[i][long]
        return at, along if at % 2 == 0 else -along

    return sorted(order, key=key)


def solution(mesh):
    devices = mesh.shape["row"]
    ring = chip_ring(mesh)

    def on_device(strain_data):
        panes, _, channels = strain_data.shape
        width = channels // devices
        fits = (
            devices % 4 == 0
            and devices >= 8
            and width % LANES == 0
            and (2 * panes * devices) % 16 == 0
        )
        if not fits:
            return gathered_form(strain_data)
        return ring_form(strain_data, ring)

    return jax.shard_map(
        on_device,
        mesh=mesh,
        in_specs=(P("row", None, "groups"),),
        out_specs=P(None, ("groups", "row"), None),
        check_vma=False,
    )
```

```python
import functools

import jax
import jax.numpy as jnp
import numpy as np
from jax import lax
from jax.experimental import pallas as pl
from jax.experimental.pallas import tpu as pltpu
from jax.sharding import PartitionSpec as P

FBIN = 5
LANES = 128
IN_VMEM = pl.BlockSpec(memory_space=pltpu.VMEM)


def project(strain_data):
    samples = strain_data.shape[1]
    position = jnp.arange(samples, dtype=jnp.float32)
    taper = 0.5 - 0.5 * jnp.cos(2.0 * jnp.pi * (position + 0.5) / samples)
    phase = 2.0 * jnp.pi * FBIN * position / samples
    weights = jnp.stack([taper * jnp.cos(phase), -taper * jnp.sin(phase)])
    rms = jnp.sqrt(jnp.mean(strain_data * strain_data, axis=1, keepdims=True))
    normed = strain_data / jnp.maximum(rms, 1.0)
    return jnp.einsum("ks,psc->kpc", weights, normed, precision=lax.Precision.HIGHEST)


def cross(left, right):
    real_part = jnp.einsum(
        "pa,pb->ab", left[0], right[0], precision=lax.Precision.HIGHEST
    ) + jnp.einsum("pa,pb->ab", left[1], right[1], precision=lax.Precision.HIGHEST)
    imag_part = jnp.einsum(
        "pa,pb->ab", left[1], right[0], precision=lax.Precision.HIGHEST
    ) - jnp.einsum("pa,pb->ab", left[0], right[1], precision=lax.Precision.HIGHEST)
    return jnp.stack([real_part, imag_part])


def gathered_form(strain_data):
    spectrum = project(strain_data)
    width = strain_data.shape[2] // lax.axis_size("row")
    offset = lax.axis_index("row") * width
    gathered = lax.all_gather(spectrum, "row", axis=1, tiled=True)
    own_rows = lax.dynamic_slice_in_dim(gathered, offset, width, 2)
    scale = lax.rsqrt(jnp.sum(gathered * gathered, axis=(0, 1)) + 1e-06)
    own_scale = lax.dynamic_slice_in_dim(scale, offset, width, 0)
    return (
        cross(own_rows, gathered) * own_scale[None, :, None] * scale[None, None, :]
    )


def tap_weights(samples):
    at = lax.broadcasted_iota(jnp.int32, (samples, LANES), 0)
    turn = 2.0 * np.pi / samples
    taper = 0.5 - 0.5 * jnp.cos((at.astype(jnp.float32) + 0.5) * turn)
    phase = ((at * FBIN) % samples).astype(jnp.float32) * turn
    return taper * jnp.cos(phase), -taper * jnp.sin(phase)


def project_kernel(strain_ref, out_ref, held, arrived):
    pieces, panes, samples, width = held.shape
    copies = [
        pltpu.make_async_copy(
            strain_ref.at[:, :, pl.ds(i * width, width)], held.at[i], arrived.at[i]
        )
        for i in range(pieces)
    ]
    for copy in copies:
        copy.start()
    weights = tap_weights(samples)
    for i in range(pieces):
        copies[i].wait()
        for lane in range(0, width, LANES):
            parts = [[], []]
            for p in range(panes):
                x = held[i, p, :, lane : lane + LANES]
                mean = jnp.sum(x * x, axis=0, keepdims=True) * (1.0 / samples)
                gain = jnp.minimum(lax.rsqrt(mean), 1.0)
                for k in range(2):
                    total = jnp.sum(x * weights[k], axis=0, keepdims=True)
                    parts[k].append(total * gain)
            at = i * width + lane
            out_ref[:, at : at + LANES] = jnp.concatenate(parts[0] + parts[1], axis=0)


def project_rows(strain_data, pieces):
    panes, samples, channels = strain_data.shape
    strain_data = pltpu.with_memory_space_constraint(strain_data, pltpu.HBM)
    return pl.pallas_call(
        project_kernel,
        in_specs=[pl.BlockSpec(memory_space=pltpu.HBM)],
        out_specs=IN_VMEM,
        scratch_shapes=[
            pltpu.VMEM((pieces, panes, samples, channels // pieces), jnp.float32),
            pltpu.SemaphoreType.DMA((pieces,)),
        ],
        out_shape=jax.ShapeDtypeStruct((2 * panes, channels), jnp.float32),
        cost_estimate=pl.CostEstimate(
            flops=6 * strain_data.size,
            bytes_accessed=4 * strain_data.size,
            transcendentals=0,
        ),
        compiler_params=pltpu.CompilerParams(vmem_limit_bytes=8 << 20),
        name="project",
    )(strain_data)


def scaled_rows(refs, block, width):
    columns = pl.ds(pl.multiple_of(block * width, width), width)
    rows = jnp.concatenate([x[:, columns] for x in refs], axis=0)
    return rows * lax.rsqrt(jnp.sum(rows * rows, axis=0, keepdims=True) + 1e-06)


def halves(x):
    high = x.astype(jnp.bfloat16)
    low = (x - high.astype(jnp.float32)).astype(jnp.bfloat16)
    return high, low


def left_operand(x, panes, part):
    if part == 1:
        count = x.shape[0]
        row = lax.broadcasted_iota(jnp.int32, x.shape, 0) % (2 * panes)
        x = jnp.where(
            row < panes, pltpu.roll(x, count - panes, 0), -pltpu.roll(x, panes, 0)
        )
    high, low = halves(jnp.concatenate([x, x], axis=0).T)
    return jnp.concatenate([high, low], axis=1)


def cross_kernel(panes, row_ref, *refs):
    *spectra, out_ref, left_ref, right_ref, held, sent = refs
    slots, parts, _, width = held.shape
    step, steps = pl.program_id(0), pl.num_programs(0)
    slot = lax.rem(step, slots)

    def store(slot, part):
        columns = pl.ds(pl.multiple_of(step * width, width), width)
        return pltpu.make_async_copy(
            held.at[slot, part], out_ref.at[part, :, columns], sent.at[slot, part]
        )

    high, low = halves(scaled_rows(spectra, step, width))
    count = high.shape[0]
    for i, half in enumerate((high, low, high, low)):
        right_ref[i * count : (i + 1) * count, :] = half
    for part in range(parts):

        @pl.when(step == 0)
        def _():
            own = scaled_rows(spectra, row_ref[0], width)
            left_ref[part] = left_operand(own, panes, part)

        @pl.when(step >= slots)
        def _():
            store(slot, part).wait()

        held[slot, part] = jnp.dot(
            left_ref[part], right_ref[...], preferred_element_type=jnp.float32
        )
        store(slot, part).start()

    @pl.when(step == steps - 1)
    def _():
        for slot in range(slots):
            for part in range(parts):
                store(slot, part).wait()


def cross_rows(row, panes, width, spectra):
    rows, columns = spectra[0].shape
    count = rows * len(spectra)
    slots = 2
    return pl.pallas_call(
        functools.partial(cross_kernel, panes),
        grid_spec=pltpu.PrefetchScalarGridSpec(
            num_scalar_prefetch=1,
            grid=(columns // width,),
            in_specs=[IN_VMEM] * len(spectra),
            out_specs=pl.BlockSpec(memory_space=pl.ANY),
            scratch_shapes=[
                pltpu.VMEM((2, width, 4 * count), jnp.bfloat16),
                pltpu.VMEM((4 * count, width), jnp.bfloat16),
                pltpu.VMEM((slots, 2, width, width), jnp.float32),
                pltpu.SemaphoreType.DMA((slots, 2)),
            ],
        ),
        out_shape=jax.ShapeDtypeStruct((2, width, columns), jnp.float32),
        cost_estimate=pl.CostEstimate(
            flops=16 * count * width * columns,
            bytes_accessed=8 * width * columns,
            transcendentals=0,
        ),
        compiler_params=pltpu.CompilerParams(vmem_limit_bytes=36 << 20),
        name="cross",
    )(row, *spectra)


def move(x, pairs):
    return lax.ppermute(x, "row", pairs)


def ring_form(strain_data, ring):
    panes, _, channels = strain_data.shape
    chips = len(ring)
    width = channels // (2 * chips)
    hop = []
    for i in range(chips):
        here, there = ring[i], ring[(i + 1) % chips]
        hop += [(2 * here, 2 * there), (2 * there + 1, 2 * here + 1)]
    swap = [(i, i ^ 1) for i in range(2 * chips)]
    row = lax.axis_index("row").astype(jnp.int32).reshape(1)

    own = project_rows(strain_data, chips)
    sibling = move(own, swap)
    spectra = [own, sibling]
    a, b = own, sibling
    for _ in range(1, (chips - 1) // 2 + 1):
        a = move(a, hop)
        b = move(b, hop)
        spectra += [a, b]
        spectra += [move(a, swap), move(b, swap)]
    tail = move(a, hop)
    spectra += [tail, move(tail, swap)]
    return cross_rows(row, panes, width, spectra)


def chip_ring(mesh):
    axes = list(mesh.axis_names)
    devices = np.moveaxis(mesh.devices, axes.index("row"), 0).reshape(
        mesh.shape["row"], -1
    )[::2, 0]
    order = list(range(len(devices)))
    if not all(hasattr(d, "coords") for d in devices):
        return order
    spots = [tuple(d.coords) for d in devices]
    varying = [a for a in range(len(spots[0])) if len({s[a] for s in spots}) > 1]
    if len(varying) != 2:
        return order
    short, long = sorted(varying, key=lambda a: len({s[a] for s in spots}))

    def key(i):
        at, along = spots[i][short], spots[i][long]
        return at, along if at % 2 == 0 else -along

    return sorted(order, key=key)


def solution(mesh):
    devices = mesh.shape["row"]
    ring = chip_ring(mesh)

    def on_device(strain_data):
        panes, _, channels = strain_data.shape
        width = channels // devices
        fits = (
            devices % 4 == 0
            and devices >= 8
            and width % LANES == 0
            and (2 * panes * devices) % 16 == 0
        )
        if not fits:
            return gathered_form(strain_data)
        return ring_form(strain_data, ring)

    return jax.shard_map(
        on_device,
        mesh=mesh,
        in_specs=(P("row", None, "groups"),),
        out_specs=P(None, ("groups", "row"), None),
        check_vma=False,
    )
```
